32 devices in a mesh: groups: 2 (over y), tm: 4 (over z), space: 2 (over x), chan: 2 (over core).
Axes of the slice: x: 2, y: 2, z: 4, core: 2. Of those that a mesh axis runs over, the one named last changes fastest.
Arguments:
- latents: bfloat16 [4, 8, 4, 8, 512], P('groups', 'tm', 'space', None, 'chan'), parts along dimension 0, may hold values from -60 to 60
- conv_weight: bfloat16 [3, 3, 3, 512, 512], P(None, None, None, 'tm', 'chan'), may hold values from -0.0546875 to 0.0546875
- conv_bias: float32 [512], P('chan'), may hold values from -4 to 4
- gn_gain: float32 [512], P('chan'), may hold values from 0.5 to 1.5
- gn_shift: float32 [512], P('chan'), may hold values from -3 to 3
- up_weight: bfloat16 [3, 3, 512, 512], P(None, None, None, 'chan'), may hold values from -0.09375 to 0.09375
- up_bias: float32 [512], P('chan'), may hold values from -3 to 3
Outputs:
- decoded: bfloat16 [4, 8, 8, 16, 512], P('groups', None, 'space', 'tm', 'chan'), parts along dimension 0
The draws below stay inside these ranges and needn't reach their ends.
There are 2 independent parts, one for each index of `groups`. The reference program is written for one: setup_inputs(seed, part) draws one part's arguments, and reference() takes and returns one part's arrays. A program takes and returns all parts, laid end to end along the dimension named above; an argument that names none is the same for every part. Nothing has to cross between parts.
All inputs are finite; a program needn't handle non-finite values.
Results may differ from the reference program's by a relative error of at most 0.0052.
The reference program's roundings to bfloat16 on the way count: a program that leaves them out, or rounds other values in their place, can miss the bound.
Values may be sent and summed in bfloat16 or wider, within the bound.
A program may use at most 64 MiB of HBM per device.

```python
import math
import jax
import jax.numpy as jnp
from jax import lax

C = 512
GROUPS = 32
TF = 2
CLIPS = 2
LATENT_FRAMES = 8
LATENT_ROWS = 4
LATENT_COLUMNS = 8


def rough_scale(key, count):
    return 10.0 ** jax.random.uniform(key, (count,), jnp.float32, 0.0, 0.25)


def shared_field(amp_key, phase_key, freq_key):
    amplitudes = jax.random.uniform(amp_key, (CLIPS, 2), jnp.float32, 1.0, 2.0)
    phases = jax.random.uniform(phase_key, (CLIPS, 2), jnp.float32, -math.pi, math.pi)
    freqs = jax.random.randint(freq_key, (CLIPS, 3), 1, 3).astype(jnp.float32)
    two_pi = 2.0 * math.pi
    frame_pos = jnp.arange(LATENT_FRAMES, dtype=jnp.float32) / LATENT_FRAMES
    row_pos = jnp.arange(LATENT_ROWS, dtype=jnp.float32) / LATENT_ROWS
    col_pos = jnp.arange(LATENT_COLUMNS, dtype=jnp.float32) / LATENT_COLUMNS
    temporal = amplitudes[:, 0, None] * jnp.cos(two_pi * freqs[:, 0, None] * frame_pos[None, :] + phases[:, 0, None])
    angle = two_pi * (freqs[:, 1, None, None] * row_pos[None, :, None] + freqs[:, 2, None, None] * col_pos[None, None, :])
    spatial = amplitudes[:, 1, None, None] * jnp.cos(angle + phases[:, 1, None, None])
    return temporal[:, :, None, None, None] + spatial[:, None, :, :, None]


def draw_latents(key, part):
    keys = jax.random.split(key, 10)
    layout = (CLIPS, LATENT_FRAMES, LATENT_ROWS, LATENT_COLUMNS, C)
    base = jax.random.truncated_normal(keys[0], -4.0, 4.0, layout, jnp.float32)
    shared = shared_field(keys[6], keys[7], keys[8])
    mixed = 0.7 * base + 0.7 * shared
    trend_frames = 2.0 ** (jnp.arange(LATENT_FRAMES, dtype=jnp.float32) / LATENT_FRAMES)
    trend_rows = 2.0 ** (jnp.arange(LATENT_ROWS, dtype=jnp.float32) / LATENT_ROWS)
    frame_scale = (trend_frames * rough_scale(keys[2], LATENT_FRAMES))[:, None, None, None]
    row_scale = (trend_rows * rough_scale(keys[3], LATENT_ROWS))[:, None, None]
    col_scale = rough_scale(keys[4], LATENT_COLUMNS)[:, None]
    upper_scale = rough_scale(keys[5], C)
    lower_scale = rough_scale(keys[9], C)
    lower_rows = jnp.arange(LATENT_ROWS) >= LATENT_ROWS // 2
    chan_scale = jnp.where(lower_rows[:, None], lower_scale[None, :], upper_scale[None, :])[:, None, :]
    scaled = mixed * frame_scale * row_scale * col_scale * chan_scale / 4.5
    return scaled.astype(jnp.bfloat16)


def block_scale(stream_key, dims, shards, least, high):
    loudness, own = 1.0, jax.random.fold_in(stream_key, 6)
    for axis_at, blocks in shards:
        draws = jnp.exp(jax.random.uniform(jax.random.fold_in(own, axis_at), (blocks,), jnp.float32, least / len(shards), high / len(shards)))
        loudness = loudness * jnp.repeat(draws, dims[axis_at] // blocks).reshape([-1 if axis == axis_at else 1 for axis in range(len(dims))])
    return loudness


def centred(stream_key, dims, width, most, pieces=(), kind=jnp.bfloat16):
    drawn = width * jax.random.normal(stream_key, dims, jnp.float32)
    if pieces:
        drawn = drawn * block_scale(stream_key, dims, pieces, -0.22, 0.18)
    return jnp.clip(drawn, -most, most).astype(kind)


def setup_inputs(seed: int = 0, part: int = 0) -> dict:
    splits = jax.random.split(jax.random.key(seed), 8)
    part_splits = jax.random.split(jax.random.fold_in(splits[7], part), 8)
    return {
        "latents": draw_latents(jax.random.fold_in(jax.random.fold_in(splits[7], part), 71), part),
        "conv_weight": centred(splits[1], (3, 3, 3, C, C), (27 * C) ** -0.5, 0.0546875, ((3, 4), (4, 2))),
        "conv_bias": centred(splits[2], (C,), 1.0, 4.0, ((0, 2),), jnp.float32),
        "gn_gain": jnp.clip(0.5 + 1.0 * jax.random.uniform(splits[3], (C,), jnp.float32) ** block_scale(splits[3], (C,), ((0, 2),), -0.2, 0.2), 0.5, 1.5),
        "gn_shift": centred(splits[4], (C,), 0.5, 3.0, ((0, 2),), jnp.float32),
        "up_weight": centred(splits[5], (3, 3, C, C), (9 * C) ** -0.5, 0.09375, ((3, 2),)),
        "up_bias": centred(splits[6], (C,), 0.5, 3.0, ((0, 2),), jnp.float32),
    }


def causal_conv(latents, conv_weight, conv_bias):
    ordered = jnp.stack([jnp.roll(latents[clip_index], -clip_index * TF, axis=0) for clip_index in range(CLIPS)])
    padded = jnp.pad(ordered.astype(jnp.float32), ((0, 0), (2, 0), (1, 1), (1, 1), (0, 0)))
    summed = lax.conv_general_dilated(padded, conv_weight.astype(jnp.float32), (1, 1, 1), 'VALID', dimension_numbers=('NDHWC', 'DHWIO', 'NDHWC'), precision=lax.Precision.HIGHEST)
    conved = (summed + conv_bias).astype(jnp.bfloat16)
    return jnp.stack([jnp.roll(conved[clip_index], clip_index * TF, axis=0) for clip_index in range(CLIPS)])

def reference(latents, conv_weight, conv_bias, gn_gain, gn_shift, up_weight, up_bias):
    conved = causal_conv(latents, conv_weight, conv_bias)
    group_width = C // GROUPS
    grouped_values = conved.astype(jnp.float32).reshape(CLIPS, LATENT_FRAMES, LATENT_ROWS, LATENT_COLUMNS, GROUPS, group_width)
    element_count = float(LATENT_FRAMES * LATENT_ROWS * LATENT_COLUMNS * group_width)
    group_mean = lax.optimization_barrier(jnp.sum(grouped_values, axis=(1, 2, 3, 5))) / element_count
    group_variance = lax.optimization_barrier(jnp.sum(grouped_values * grouped_values, axis=(1, 2, 3, 5))) / element_count - group_mean * group_mean
    factor = lax.rsqrt(group_variance + 1e-06)
    normed = (grouped_values - group_mean[:, None, None, None, :, None]) * factor[:, None, None, None, :, None]
    normed = normed.reshape(CLIPS, LATENT_FRAMES, LATENT_ROWS, LATENT_COLUMNS, C) * gn_gain + gn_shift
    active = jax.nn.silu(normed).astype(jnp.bfloat16)
    widened = jnp.repeat(jnp.repeat(active, 2, axis=2), 2, axis=3)
    padded = jnp.pad(widened.astype(jnp.float32), ((0, 0), (0, 0), (1, 1), (1, 1), (0, 0)))
    flat = padded.reshape(CLIPS * LATENT_FRAMES, 2 * LATENT_ROWS + 2, 2 * LATENT_COLUMNS + 2, C)
    output = lax.conv_general_dilated(flat, up_weight.astype(jnp.float32), (1, 1), 'VALID', dimension_numbers=('NHWC', 'HWIO', 'NHWC'), precision=lax.Precision.HIGHEST)
    output = output + up_bias
    return output.reshape(CLIPS, LATENT_FRAMES, 2 * LATENT_ROWS, 2 * LATENT_COLUMNS, C).astype(jnp.bfloat16)
```

```python
import functools

import jax
import jax.numpy as jnp
import numpy as np
from jax import lax
from jax.experimental import pallas as pl
from jax.experimental.pallas import tpu as pltpu
from jax.sharding import PartitionSpec as P

C = 512
GROUPS = 32


def from_behind(value, axis, steps):
    count = lax.axis_size(axis)
    pairs = [(source, (source + steps) % count) for source in range(count)]
    return lax.ppermute(value, axis, pairs)


def with_halo(block, sides, width):
    for axis, dim in sides:
        count = lax.axis_size(axis)
        forward = [(i, i + 1) for i in range(count - 1)]
        backward = [(target, source) for source, target in forward]
        low = lax.ppermute(
            lax.slice_in_dim(block, block.shape[dim] - width, None, axis=dim), axis, forward
        )
        high = lax.ppermute(lax.slice_in_dim(block, 0, width, axis=dim), axis, backward)
        block = jnp.concatenate([low, block, high], axis=dim)
    return block


def causal_frames(latents):
    clip_count = latents.shape[0]
    span_count = lax.axis_size("tm")
    span_index = lax.axis_index("tm")
    tail_frames = from_behind(latents, "tm", 1)
    clip_order = jnp.arange(clip_count, dtype=jnp.int32)
    opening = (span_index - clip_order) % span_count == 0
    tail_frames = jnp.where(
        opening[:, None, None, None, None], jnp.zeros_like(tail_frames), tail_frames
    )
    return jnp.concatenate([tail_frames, latents], axis=1)


def causal_conv(latents, conv_weight, conv_bias):
    framed = causal_frames(latents)
    bordered = with_halo(framed, (("space", 2),), 1)
    gathered = lax.all_gather(bordered, "chan", axis=4, tiled=True)
    padded = jnp.pad(gathered, ((0, 0), (0, 0), (0, 0), (1, 1), (0, 0)))
    initial = jnp.zeros(latents.shape[:4] + (conv_weight.shape[4],), jnp.float32)
    summed = initial + lax.conv_general_dilated(
        padded,
        lax.all_gather(conv_weight, "tm", axis=3, tiled=True),
        (1, 1, 1),
        "VALID",
        dimension_numbers=("NDHWC", "DHWIO", "NDHWC"),
        preferred_element_type=jnp.float32,
    )
    return (summed + conv_bias).astype(jnp.bfloat16)


def moments(block):
    clip_count, frame_count, row_count, col_count, chan_count = block.shape
    group_width = C // GROUPS
    grouped_values = block.astype(jnp.float32).reshape(
        clip_count, frame_count, row_count, col_count, chan_count // group_width, group_width
    )
    group_sums = jnp.sum(grouped_values, axis=(1, 2, 3, 5))
    squared_sums = jnp.sum(grouped_values * grouped_values, axis=(1, 2, 3, 5))
    group_sums, squared_sums = lax.psum((group_sums, squared_sums), ("tm", "space"))
    element_count = float(
        frame_count
        * row_count
        * col_count
        * group_width
        * lax.axis_size("tm")
        * lax.axis_size("space")
    )
    group_mean = group_sums / element_count
    group_variance = squared_sums / element_count - group_mean * group_mean
    return (group_mean, lax.rsqrt(group_variance + 1e-06))


def activate(block, group_mean, factor, gn_gain, gn_shift):
    clip_count, frame_count, row_count, col_count, chan_count = block.shape
    group_width = C // GROUPS
    grouped_values = block.astype(jnp.float32).reshape(
        clip_count, frame_count, row_count, col_count, chan_count // group_width, group_width
    )
    normed = (grouped_values - group_mean[:, None, None, None, :, None]) * factor[
        :, None, None, None, :, None
    ]
    normed = normed.reshape(block.shape) * gn_gain + gn_shift
    return jax.nn.silu(normed).astype(jnp.bfloat16)


def relayout(block):
    return lax.all_to_all(block, "tm", split_axis=3, concat_axis=1, tiled=True)


def widen(rimmed, up_weight, up_bias):
    gathered = lax.all_gather(rimmed, "chan", axis=4, tiled=True)
    widened = jnp.repeat(jnp.repeat(gathered, 2, axis=2), 2, axis=3)[:, :, 1:-1, 1:-1]
    clip_count, frame_count, tall_count, broad_count, depth_count = widened.shape
    flat = widened.reshape(clip_count * frame_count, tall_count, broad_count, depth_count)
    output = lax.conv_general_dilated(
        flat,
        up_weight,
        (1, 1),
        "VALID",
        dimension_numbers=("NHWC", "HWIO", "NHWC"),
        preferred_element_type=jnp.float32,
    )
    output = output + up_bias
    return output.reshape(
        clip_count, frame_count, tall_count - 2, broad_count - 2, up_weight.shape[3]
    ).astype(jnp.bfloat16)


def on_device(latents, conv_weight, conv_bias, gn_gain, gn_shift, up_weight, up_bias):
    conved = causal_conv(latents, conv_weight, conv_bias)
    tiled = relayout(conved)
    group_mean, factor = moments(tiled)
    active = activate(tiled, group_mean, factor, gn_gain, gn_shift)
    rimmed = with_halo(active, (("tm", 3), ("space", 2)), 1)
    return widen(rimmed, up_weight, up_bias)


MESH = pl.DeviceIdType.MESH
SEND = jnp.bfloat16


def gather_matrix(clips, spans, per, cols):
    frames = spans * per
    pick = np.zeros((3, cols, clips, frames, spans, clips, per, cols), np.float32)
    for a in range(3):
        for col in range(cols):
            for c in range(clips):
                for k in range(2 - a, frames):
                    slot = (k - 2 + a + c * per) % frames
                    pick[a, col, c, (k + c * per) % frames, slot // per, c, slot % per, col] = 1.0
    return pick.reshape(3, cols * clips * frames, spans * clips * per * cols)


def fused(sizes, x_ref, pick_hbm, bias_hbm, gain_hbm, shift_hbm, upb_hbm, w_hbm, up_hbm, out_ref,
          pick_ref, vecs, wv, upv, rx, fr, kept, sb, rb, halo, act, st, par, lsem, s1, r1, s2, r2, s3, r3, s4, r4, s5, r5):
    T, R, TC, CL, FR = sizes
    g, t, s, c = (lax.axis_index(n) for n in ("groups", "tm", "space", "chan"))
    cin = rx.shape[-1]
    Q = x_ref.shape[-1] // cin
    other = 1 - s
    wcopy = pltpu.make_async_copy(w_hbm, wv, lsem.at[0])
    upcopy = pltpu.make_async_copy(up_hbm, upv, lsem.at[1])
    pcopy = pltpu.make_async_copy(pick_hbm, pick_ref, lsem.at[2])
    vcopies = [
        pltpu.make_async_copy(ref, vecs.at[k], lsem.at[3 + k])
        for k, ref in enumerate((bias_hbm, gain_hbm, shift_hbm, upb_hbm))
    ]
    barrier = pltpu.get_barrier_semaphore()
    for dt in range(T):
        for ds in range(2):
            for dc in range(2):
                if dt or ds or dc:
                    pl.semaphore_signal(
                        barrier, inc=1,
                        device_id=(g, lax.rem(t + dt, T), lax.rem(s + ds, 2), lax.rem(c + dc, 2)),
                        device_id_type=MESH,
                    )
    pcopy.start()
    wcopy.start()
    for copy in vcopies:
        copy.start()
    edge = s * (R + 1)
    rx[:, :, :, pl.ds(edge, 1)] = jnp.zeros(rx.shape[:3] + (1,) + rx.shape[4:], rx.dtype)
    W = fr.shape[1] - 2
    for col in (0, W + 1):
        fr[:, col] = jnp.zeros((3,) + fr.shape[2:], fr.dtype)
    pl.semaphore_wait(barrier, 4 * T - 1)

    sends = []
    for q in range(Q):
        lanes = pl.ds(q * cin, cin)
        target = c * Q + q
        for dc in range(2):
            to_core = lax.rem(c + dc, 2)
            near = pltpu.make_async_remote_copy(
                src_ref=x_ref.at[:, :, :, :, lanes], dst_ref=rx.at[t, :, :, pl.ds(1, R)],
                send_sem=s1.at[q, dc, 0], recv_sem=r1.at[0, t],
                device_id=(g, target, s, to_core), device_id_type=MESH)
            far = pltpu.make_async_remote_copy(
                src_ref=x_ref.at[:, :, pl.ds((1 - s) * (R - 1), 1), :, lanes],
                dst_ref=rx.at[t, :, :, pl.ds((1 - other) * (R + 1), 1)],
                send_sem=s1.at[q, dc, 1], recv_sem=r1.at[1, t],
                device_id=(g, target, other, to_core), device_id_type=MESH)
            far.start()
            sends.append((far, None))
            if dc:
                near.start()
                sends.append((near, None))
            else:
                local = pltpu.make_async_copy(
                    x_ref.at[:, :, :, :, lanes], rx.at[t, :, :, pl.ds(1, R)], r1.at[0, t])
                pl.when(target == t)(local.start)
                pl.when(target != t)(near.start)
                sends.append((near, target != t))
    upcopy.start()
    for k, ref in enumerate((gain_hbm, shift_hbm)):
        copy = pltpu.make_async_remote_copy(
            src_ref=ref, dst_ref=par.at[k], send_sem=s5.at[k], recv_sem=r5.at[k],
            device_id=(g, t, s, 1 - c), device_id_type=MESH)
        copy.start()
        sends.append((copy, None))
    pcopy.wait()
    wcopy.wait()
    for copy in vcopies:
        copy.wait()
    for source in range(T):
        for kind, rows in ((0, pl.ds(1, R)), (1, pl.ds((1 - s) * (R + 1), 1))):
            dst = rx.at[source, :, :, rows]
            pltpu.make_async_copy(dst, dst, r1.at[kind, source]).wait()

    stacked = jnp.concatenate([rx[:, :, :, r].reshape(-1, cin) for r in range(R + 2)], axis=1)
    frames = CL * FR
    for a in range(3):
        picked = jnp.dot(pick_ref[a], stacked, preferred_element_type=jnp.float32)
        fr[a, 1:W + 1] = picked.astype(fr.dtype).reshape(W, frames, stacked.shape[1])
    taps = wv.shape[0] * wv.shape[1] * wv.shape[2]
    half = W // 2

    def send(step, u):
        side = lax.rem(t // 2 + 1 + step, 2)
        to = 3 * side if u == 0 else 1 + side
        return to, pltpu.make_async_remote_copy(
            src_ref=sb.at[to], dst_ref=rb.at[t], send_sem=s2.at[step, u], recv_sem=r2.at[t],
            device_id=(g, to, s, c), device_id_type=MESH)

    def halfway(step, carry):
        side = lax.rem(t // 2 + 1 + step, 2)
        lhs = jnp.concatenate([
            jnp.concatenate([
                fr[a, pl.ds(side * half + e, half), :, (r + b) * cin:(r + b + 1) * cin].reshape(half * frames, cin)
                for r in range(R)], axis=0)
            for a in range(3) for b in range(3) for e in range(3)], axis=1)
        total = jnp.dot(lhs, wv[...].reshape(taps * cin, wv.shape[4]), preferred_element_type=jnp.float32)
        parts = total.reshape(R, 2, TC * frames, wv.shape[4])
        kept[...] = parts
        for u in range(2):
            sb[side * 2 + u] = parts[:, u].astype(sb.dtype)
        for u in range(2):
            to, copy = send(step, u)
            pl.when(to != t)(copy.start)
        return carry

    lax.fori_loop(0, 2, halfway, 0)
    for step in range(2):
        for u in range(2):
            to, copy = send(step, u)
            sends.append((copy, to != t))
    summed = kept[:, lax.rem(t, 2)]
    for dt in (1, 3, 2):
        source = lax.rem(t + dt, T)
        pltpu.make_async_copy(rb.at[source], rb.at[source], r2.at[source]).wait()
        summed = summed + rb[source].astype(jnp.float32)
    summed = summed.reshape(R * TC * frames, wv.shape[4])
    conved = (summed + vecs[0]).astype(jnp.bfloat16)
    CO = conved.shape[1]
    halo[c, 1:R + 1, 1:TC + 1] = conved.reshape(R, TC, frames, CO)

    rims = []
    for dt in (0, -1, 1):
        for ds in range(2):
            for dc in range(2):
                if not (dt or ds or dc):
                    continue
                rows_src = pl.ds(1, R) if ds == 0 else pl.ds(1 + (1 - s) * (R - 1), 1)
                rows_dst = pl.ds(1, R) if ds == 0 else pl.ds((1 - other) * (R + 1), 1)
                rows_in = pl.ds(1, R) if ds == 0 else pl.ds((1 - s) * (R + 1), 1)
                cols_src = pl.ds(1, TC) if dt == 0 else pl.ds(TC if dt == 1 else 1, 1)
                cols_dst = pl.ds(1, TC) if dt == 0 else pl.ds(0 if dt == 1 else TC + 1, 1)
                core = lax.rem(c + dc, 2)
                copy = pltpu.make_async_remote_copy(
                    src_ref=halo.at[c, rows_src, cols_src], dst_ref=halo.at[c, rows_dst, cols_dst],
                    send_sem=s3.at[dt + 1, ds, dc], recv_sem=r3.at[dt + 1, ds, dc],
                    device_id=(g, jnp.clip(t + dt, 0, T - 1) if dt else t, s if ds == 0 else other, core),
                    device_id_type=MESH)
                there = None if dt == 0 else (t < T - 1 if dt == 1 else t > 0)
                came = None if dt == 0 else (t > 0 if dt == 1 else t < T - 1)
                landed = halo.at[core, rows_in, cols_dst]
                arrival = pltpu.make_async_copy(landed, landed, r3.at[dt + 1, ds, dc])
                rims.append((copy, there, arrival, came))

    values = conved.astype(jnp.float32).reshape(R * TC, CL, FR, CO)
    firsts = jnp.sum(jnp.sum(values, axis=0), axis=1)
    seconds = jnp.sum(jnp.sum(values * values, axis=0), axis=1)
    stats = jnp.concatenate([firsts, seconds], axis=0)
    width = C // GROUPS
    local = CO // width
    fold = (lax.broadcasted_iota(jnp.int32, (CO, 128), 0) // width
            == lax.broadcasted_iota(jnp.int32, (CO, 128), 1) % local).astype(jnp.float32)
    spread = (lax.broadcasted_iota(jnp.int32, (128, CO), 1) // width
              == lax.broadcasted_iota(jnp.int32, (128, CO), 0) % local).astype(jnp.float32)
    lane = lax.broadcasted_iota(jnp.int32, (2 * CL, 128), 1) // local
    kind = lax.broadcasted_iota(jnp.int32, (2 * CL, 128), 0)
    folded = jnp.dot(stats, fold, precision=lax.Precision.HIGHEST, preferred_element_type=jnp.float32)
    st[c, s * T + t] = jnp.sum(jnp.where(lane == kind, folded, 0.0), axis=0, keepdims=True)
    for dt in range(T):
        for ds in range(2):
            for dc in range(2):
                if dt or ds or dc:
                    copy = pltpu.make_async_remote_copy(
                        src_ref=st.at[c, s * T + t], dst_ref=st.at[c, s * T + t],
                        send_sem=s4.at[dt, ds, dc], recv_sem=r4.at[c, s * T + t],
                        device_id=(g, lax.rem(t + dt, T), lax.rem(s + ds, 2), lax.rem(c + dc, 2)),
                        device_id_type=MESH)
                    copy.start()
                    sends.append((copy, None))
    for copy, there, _, _ in rims:
        if there is None:
            copy.start()
        else:
            pl.when(there)(copy.start)
        sends.append((copy, there))
    for dt in range(T):
        for ds in range(2):
            for dc in range(2):
                if dt or ds or dc:
                    core = lax.rem(c + dc, 2)
                    place = lax.rem(s + ds, 2) * T + lax.rem(t + dt, T)
                    pltpu.make_async_copy(st.at[core, place], st.at[core, place], r4.at[core, place]).wait()
    for k in range(2):
        pltpu.make_async_copy(par.at[k], par.at[k], r5.at[k]).wait()
    for _, _, arrival, came in rims:
        if came is None:
            arrival.wait()
        else:
            pl.when(came)(arrival.wait)

    count = float(2 * T * R * TC * FR * width)
    row_at = lax.broadcasted_iota(jnp.int32, (R + 2, TC + 2, CL, FR, CO), 0)
    col_at = lax.broadcasted_iota(jnp.int32, (R + 2, TC + 2, CL, FR, CO), 1)
    outside = (row_at == edge) | ((col_at == 0) & (t == 0)) | ((col_at == TC + 1) & (t == T - 1))
    for core in range(2):
        sums = st[core, 0]
        for k in range(1, 2 * T):
            sums = sums + st[core, k]
        mean = sums / count
        squares = pltpu.roll(jnp.broadcast_to(mean, (8, 128)), 128 - CL * local, axis=1)[:1]
        factor = lax.rsqrt(squares - mean * mean + 1e-06)
        rows = jnp.where(kind < CL, jnp.broadcast_to(mean, kind.shape), jnp.broadcast_to(factor, kind.shape))
        both = jnp.dot(jnp.where(lane == kind % CL, rows, 0.0), spread,
                       precision=lax.Precision.HIGHEST, preferred_element_type=jnp.float32)
        here = c == core
        gain = jnp.where(here, vecs[1], par[0])
        shift = jnp.where(here, vecs[2], par[1])
        block_in = halo[core].astype(jnp.float32).reshape(R + 2, TC + 2, CL, FR, CO)
        v = (block_in - both[:CL][None, None, :, None, :]) * both[CL:][None, None, :, None, :]
        v = v * gain.reshape(1, 1, 1, 1, CO) + shift.reshape(1, 1, 1, 1, CO)
        v = jnp.where(outside, 0.0, v / (1.0 + jnp.exp(-v)))
        act[:, :, :, core * CO:(core + 1) * CO] = v.reshape(R + 2, TC + 2, frames, CO).astype(jnp.bfloat16)

    upcopy.wait()
    across = {}
    for b in range(3):
        rows = sorted({(i + b + 1) // 2 for i in range(2 * R)})
        for e in range(3):
            cols = sorted({(j + e + 1) // 2 for j in range(2 * TC)})
            lhs = jnp.concatenate([act[r, q] for r in rows for q in cols], axis=0)
            term = jnp.dot(lhs, upv[b, e], preferred_element_type=jnp.float32)
            term = term.reshape(len(rows), len(cols), frames, CO)
            for k, r in enumerate(rows):
                for j in range(2 * TC):
                    piece = term[k, cols.index((j + e + 1) // 2)]
                    across[b, r, j] = piece if e == 0 else across[b, r, j] + piece
    total = jnp.concatenate([
        across[0, (i + 1) // 2, j] + across[1, (i + 2) // 2, j] + across[2, (i + 3) // 2, j]
        for i in range(2 * R) for j in range(2 * TC)], axis=0)
    rounded = (total + vecs[3]).astype(jnp.bfloat16)
    out_ref[...] = rounded
    for copy, there in sends:
        if there is None:
            copy.wait_send()
        else:
            pl.when(there)(copy.wait_send)


def in_one_kernel(latents, conv_weight, conv_bias, gn_gain, gn_shift, up_weight, up_bias):
    T = lax.axis_size("tm")
    CL, per, R, W, depth = latents.shape
    cin, CO = conv_weight.shape[3:]
    TC, FR = W // T, T * per
    frames = CL * FR
    pick = jnp.asarray(gather_matrix(CL, T, per, W), jnp.bfloat16)
    rows = [v.reshape(1, CO) for v in (conv_bias, gn_gain, gn_shift, up_bias)]
    dma, vmem, anywhere = pltpu.SemaphoreType.DMA, pl.BlockSpec(memory_space=pltpu.VMEM), pl.BlockSpec(memory_space=pl.ANY)
    out = pl.pallas_call(
        functools.partial(fused, (T, R, TC, CL, FR)),
        out_shape=pltpu.VMEM((4 * R * TC * frames, CO), jnp.bfloat16),
        in_specs=[anywhere] * 8,
        out_specs=vmem,
        scratch_shapes=[
            pltpu.VMEM(pick.shape, jnp.bfloat16),
            pltpu.VMEM((4, 1, CO), jnp.float32),
            pltpu.VMEM(conv_weight.shape, jnp.bfloat16),
            pltpu.VMEM(up_weight.shape, jnp.bfloat16),
            pltpu.VMEM((T, CL, per, R + 2, W, cin), jnp.bfloat16),
            pltpu.VMEM((3, W + 2, frames, (R + 2) * cin), jnp.bfloat16),
            pltpu.VMEM((R, 2, TC * frames, CO), jnp.float32),
            pltpu.VMEM((T, R, TC * frames, CO), SEND),
            pltpu.VMEM((T, R, TC * frames, CO), SEND),
            pltpu.VMEM((2, R + 2, TC + 2, frames, CO), jnp.bfloat16),
            pltpu.VMEM((R + 2, TC + 2, frames, C), jnp.bfloat16),
            pltpu.VMEM((2, 2 * T, 1, 128), jnp.float32),
            pltpu.VMEM((2, 1, CO), jnp.float32),
            dma((7,)),
            dma((depth // cin, 2, 2)), dma((2, T)),
            dma((2, 2)), dma((T,)),
            dma((3, 2, 2)), dma((3, 2, 2)),
            dma((T, 2, 2)), dma((2, 2 * T)),
            dma((2,)), dma((2,)),
        ],
        compiler_params=pltpu.CompilerParams(collective_id=0, has_side_effects=True),
    )(latents, pick, *rows, conv_weight, up_weight)
    return out.reshape(2 * R, 2 * TC, CL, FR, CO).transpose(2, 3, 0, 1, 4)


def chosen(*operands):
    latents, conv_weight = operands[:2]
    T = lax.axis_size("tm")
    fits = (
        lax.axis_size("space") == 2 and lax.axis_size("chan") == 2 and T == 4 and latents.shape[0] == 2
        and conv_weight.shape[3] % 128 == 0 and T * latents.shape[1] == 8 and conv_weight.shape[4] == 256 and latents.shape[3] % T == 0
    )
    return (in_one_kernel if fits else on_device)(*operands)


def solution(mesh):
    placed = (
        P("groups", "tm", "space", None, "chan"),
        P(None, None, None, "tm", "chan"),
        P("chan"),
        P("chan"),
        P("chan"),
        P(None, None, None, "chan"),
        P("chan"),
    )
    return jax.shard_map(
        chosen,
        mesh=mesh,
        in_specs=placed,
        out_specs=P("groups", None, "space", "tm", "chan"),
        check_vma=False,
    )
```

```python
import functools

import jax
import jax.numpy as jnp
import numpy as np
from jax import lax
from jax.experimental import pallas as pl
from jax.experimental.pallas import tpu as pltpu
from jax.sharding import PartitionSpec as P

C = 512
GROUPS = 32


def from_behind(value, axis, steps):
    count = lax.axis_size(axis)
    pairs = [(source, (source + steps) % count) for source in range(count)]
    return lax.ppermute(value, axis, pairs)


def with_halo(block, sides, width):
    for axis, dim in sides:
        count = lax.axis_size(axis)
        forward = [(i, i + 1) for i in range(count - 1)]
        backward = [(target, source) for source, target in forward]
        low = lax.ppermute(
            lax.slice_in_dim(block, block.shape[dim] - width, None, axis=dim), axis, forward
        )
        high = lax.ppermute(lax.slice_in_dim(block, 0, width, axis=dim), axis, backward)
        block = jnp.concatenate([low, block, high], axis=dim)
    return block


def causal_frames(latents):
    clip_count = latents.shape[0]
    span_count = lax.axis_size("tm")
    span_index = lax.axis_index("tm")
    tail_frames = from_behind(latents, "tm", 1)
    clip_order = jnp.arange(clip_count, dtype=jnp.int32)
    opening = (span_index - clip_order) % span_count == 0
    tail_frames = jnp.where(
        opening[:, None, None, None, None], jnp.zeros_like(tail_frames), tail_frames
    )
    return jnp.concatenate([tail_frames, latents], axis=1)


def causal_conv(latents, conv_weight, conv_bias):
    framed = causal_frames(latents)
    bordered = with_halo(framed, (("space", 2),), 1)
    gathered = lax.all_gather(bordered, "chan", axis=4, tiled=True)
    padded = jnp.pad(gathered, ((0, 0), (0, 0), (0, 0), (1, 1), (0, 0)))
    initial = jnp.zeros(latents.shape[:4] + (conv_weight.shape[4],), jnp.float32)
    summed = initial + lax.conv_general_dilated(
        padded,
        lax.all_gather(conv_weight, "tm", axis=3, tiled=True),
        (1, 1, 1),
        "VALID",
        dimension_numbers=("NDHWC", "DHWIO", "NDHWC"),
        preferred_element_type=jnp.float32,
    )
    return (summed + conv_bias).astype(jnp.bfloat16)


def moments(block):
    clip_count, frame_count, row_count, col_count, chan_count = block.shape
    group_width = C // GROUPS
    grouped_values = block.astype(jnp.float32).reshape(
        clip_count, frame_count, row_count, col_count, chan_count // group_width, group_width
    )
    group_sums = jnp.sum(grouped_values, axis=(1, 2, 3, 5))
    squared_sums = jnp.sum(grouped_values * grouped_values, axis=(1, 2, 3, 5))
    group_sums, squared_sums = lax.psum((group_sums, squared_sums), ("tm", "space"))
    element_count = float(
        frame_count
        * row_count
        * col_count
        * group_width
        * lax.axis_size("tm")
        * lax.axis_size("space")
    )
    group_mean = group_sums / element_count
    group_variance = squared_sums / element_count - group_mean * group_mean
    return (group_mean, lax.rsqrt(group_variance + 1e-06))


def activate(block, group_mean, factor, gn_gain, gn_shift):
    clip_count, frame_count, row_count, col_count, chan_count = block.shape
    group_width = C // GROUPS
    grouped_values = block.astype(jnp.float32).reshape(
        clip_count, frame_count, row_count, col_count, chan_count // group_width, group_width
    )
    normed = (grouped_values - group_mean[:, None, None, None, :, None]) * factor[
        :, None, None, None, :, None
    ]
    normed = normed.reshape(block.shape) * gn_gain + gn_shift
    return jax.nn.silu(normed).astype(jnp.bfloat16)


def relayout(block):
    return lax.all_to_all(block, "tm", split_axis=3, concat_axis=1, tiled=True)


def widen(rimmed, up_weight, up_bias):
    gathered = lax.all_gather(rimmed, "chan", axis=4, tiled=True)
    widened = jnp.repeat(jnp.repeat(gathered, 2, axis=2), 2, axis=3)[:, :, 1:-1, 1:-1]
    clip_count, frame_count, tall_count, broad_count, depth_count = widened.shape
    flat = widened.reshape(clip_count * frame_count, tall_count, broad_count, depth_count)
    output = lax.conv_general_dilated(
        flat,
        up_weight,
        (1, 1),
        "VALID",
        dimension_numbers=("NHWC", "HWIO", "NHWC"),
        preferred_element_type=jnp.float32,
    )
    output = output + up_bias
    return output.reshape(
        clip_count, frame_count, tall_count - 2, broad_count - 2, up_weight.shape[3]
    ).astype(jnp.bfloat16)


def on_device(latents, conv_weight, conv_bias, gn_gain, gn_shift, up_weight, up_bias):
    conved = causal_conv(latents, conv_weight, conv_bias)
    tiled = relayout(conved)
    group_mean, factor = moments(tiled)
    active = activate(tiled, group_mean, factor, gn_gain, gn_shift)
    rimmed = with_halo(active, (("tm", 3), ("space", 2)), 1)
    return widen(rimmed, up_weight, up_bias)


MESH = pl.DeviceIdType.MESH
SEND = jnp.bfloat16


def gather_matrix(clips, spans, per, cols):
    frames = spans * per
    pick = np.zeros((3, cols, clips, frames, spans, clips, per, cols), np.float32)
    for a in range(3):
        for col in range(cols):
            for c in range(clips):
                for k in range(2 - a, frames):
                    slot = (k - 2 + a + c * per) % frames
                    pick[a, col, c, (k + c * per) % frames, slot // per, c, slot % per, col] = 1.0
    return pick.reshape(3, cols * clips * frames, spans * clips * per * cols)


def thirds(value):
    high = value.astype(jnp.bfloat16)
    rest = value - high.astype(jnp.float32)
    middle = rest.astype(jnp.bfloat16)
    low = (rest - middle.astype(jnp.float32)).astype(jnp.bfloat16)
    return high, middle, low


def fused(sizes, x_ref, pick_hbm, bias_hbm, gain_hbm, shift_hbm, upb_hbm, w_hbm, up_hbm, out_ref,
          pick_ref, vecs, wv, upv, rx, fr, kept, sb, rb, halo, act, st, par, lsem, s1, r1, s2, r2, s3, r3, s4, r4, s5, r5):
    T, R, TC, CL, FR = sizes
    g, t, s, c = (lax.axis_index(n) for n in ("groups", "tm", "space", "chan"))
    cin = rx.shape[-1]
    Q = x_ref.shape[-1] // cin
    other = 1 - s
    wcopy = pltpu.make_async_copy(w_hbm, wv, lsem.at[0])
    upcopy = pltpu.make_async_copy(up_hbm, upv, lsem.at[1])
    pcopy = pltpu.make_async_copy(pick_hbm, pick_ref, lsem.at[2])
    vcopies = [
        pltpu.make_async_copy(ref, vecs.at[k], lsem.at[3 + k])
        for k, ref in enumerate((bias_hbm, gain_hbm, shift_hbm, upb_hbm))
    ]
    barrier = pltpu.get_barrier_semaphore()
    for dt in (1, 2, 3, 0):
        for ds in (1, 0):
            for dc in range(2):
                if dt or ds or dc:
                    pl.semaphore_signal(
                        barrier, inc=1,
                        device_id=(g, lax.rem(t + dt, T), lax.rem(s + ds, 2), lax.rem(c + dc, 2)),
                        device_id_type=MESH,
                    )
    pcopy.start()
    wcopy.start()
    for copy in vcopies:
        copy.start()
    edge = s * (R + 1)
    rx[:, :, :, pl.ds(edge, 1)] = jnp.zeros(rx.shape[:3] + (1,) + rx.shape[4:], rx.dtype)
    W = fr.shape[1] - 2
    for col in (0, W + 1):
        fr[:, col] = jnp.zeros((3,) + fr.shape[2:], fr.dtype)
    pl.semaphore_wait(barrier, 4 * T - 1)

    sends = []
    first = jnp.where(t <= 2 * c, 1, 0)
    for turn in range(Q):
        q = first if turn == 0 else 1 - first
        lanes = pl.ds(pl.multiple_of(q * cin, cin), cin)
        target = c * Q + q
        for dc in range(2):
            far = pltpu.make_async_remote_copy(
                src_ref=x_ref.at[:, :, pl.ds((1 - s) * (R - 1), 1), :, lanes],
                dst_ref=rx.at[t, :, :, pl.ds((1 - other) * (R + 1), 1)],
                send_sem=s1.at[turn, dc, 1], recv_sem=r1.at[1, t],
                device_id=(g, target, other, lax.rem(c + dc, 2)), device_id_type=MESH)
            far.start()
            sends.append((far, None))
        for dc in range(2):
            near = pltpu.make_async_remote_copy(
                src_ref=x_ref.at[:, :, :, :, lanes], dst_ref=rx.at[t, :, :, pl.ds(1, R)],
                send_sem=s1.at[turn, dc, 0], recv_sem=r1.at[0, t],
                device_id=(g, target, s, lax.rem(c + dc, 2)), device_id_type=MESH)
            if dc:
                near.start()
                sends.append((near, None))
            else:
                local = pltpu.make_async_copy(
                    x_ref.at[:, :, :, :, lanes], rx.at[t, :, :, pl.ds(1, R)], r1.at[0, t])
                pl.when(target == t)(local.start)
                pl.when(target != t)(near.start)
                sends.append((near, target != t))
    upcopy.start()
    for k, ref in enumerate((gain_hbm, shift_hbm)):
        copy = pltpu.make_async_remote_copy(
            src_ref=ref, dst_ref=par.at[k], send_sem=s5.at[k], recv_sem=r5.at[k],
            device_id=(g, t, s, 1 - c), device_id_type=MESH)
        copy.start()
        sends.append((copy, None))
    pcopy.wait()
    wcopy.wait()
    for copy in vcopies:
        copy.wait()
    for source in range(T):
        for kind, rows in ((0, pl.ds(1, R)), (1, pl.ds((1 - s) * (R + 1), 1))):
            dst = rx.at[source, :, :, rows]
            pltpu.make_async_copy(dst, dst, r1.at[kind, source]).wait()

    stacked = jnp.concatenate([rx[:, :, :, r].reshape(-1, cin) for r in range(R + 2)], axis=1)
    frames = CL * FR
    for a in range(3):
        picked = jnp.dot(pick_ref[a], stacked, preferred_element_type=jnp.float32)
        fr[a, 1:W + 1] = picked.astype(fr.dtype).reshape(W, frames, stacked.shape[1])
    taps = wv.shape[0] * wv.shape[1] * wv.shape[2]
    half = W // 2

    def send(step, u):
        side = lax.rem(t // 2 + 1 + step, 2)
        to = 3 * side if u == 0 else 1 + side
        return to, pltpu.make_async_remote_copy(
            src_ref=sb.at[to], dst_ref=rb.at[t], send_sem=s2.at[step, u], recv_sem=r2.at[t],
            device_id=(g, to, s, c), device_id_type=MESH)

    def halfway(step, carry):
        side = lax.rem(t // 2 + 1 + step, 2)
        lhs = jnp.concatenate([
            jnp.concatenate([
                fr[a, pl.ds(side * half + e, half), :, (r + b) * cin:(r + b + 1) * cin].reshape(half * frames, cin)
                for r in range(R)], axis=0)
            for a in range(3) for b in range(3) for e in range(3)], axis=1)
        total = jnp.dot(lhs, wv[...].reshape(taps * cin, wv.shape[4]), preferred_element_type=jnp.float32)
        parts = total.reshape(R, 2, TC * frames, wv.shape[4])
        kept[...] = parts
        for u in range(2):
            sb[side * 2 + u] = parts[:, u].astype(sb.dtype)
        for u in range(2):
            to, copy = send(step, u)
            pl.when(to != t)(copy.start)
        return carry

    lax.fori_loop(0, 2, halfway, 0)
    for step in range(2):
        for u in range(2):
            to, copy = send(step, u)
            sends.append((copy, to != t))
    summed = kept[:, lax.rem(t, 2)]
    for dt in (1, 3, 2):
        source = lax.rem(t + dt, T)
        pltpu.make_async_copy(rb.at[source], rb.at[source], r2.at[source]).wait()
        summed = summed + rb[source].astype(jnp.float32)
    summed = summed.reshape(R * TC * frames, wv.shape[4])
    conved = (summed + vecs[0]).astype(jnp.bfloat16)
    CO = conved.shape[1]
    halo[c, 1:R + 1, 1:TC + 1] = conved.reshape(R, TC, frames, CO)

    rims = []
    for dt in (0, -1, 1):
        for ds in range(2):
            for dc in range(2):
                if not (dt or ds or dc):
                    continue
                rows_src = pl.ds(1, R) if ds == 0 else pl.ds(1 + (1 - s) * (R - 1), 1)
                rows_dst = pl.ds(1, R) if ds == 0 else pl.ds((1 - other) * (R + 1), 1)
                rows_in = pl.ds(1, R) if ds == 0 else pl.ds((1 - s) * (R + 1), 1)
                cols_src = pl.ds(1, TC) if dt == 0 else pl.ds(TC if dt == 1 else 1, 1)
                cols_dst = pl.ds(1, TC) if dt == 0 else pl.ds(0 if dt == 1 else TC + 1, 1)
                core = lax.rem(c + dc, 2)
                copy = pltpu.make_async_remote_copy(
                    src_ref=halo.at[c, rows_src, cols_src], dst_ref=halo.at[c, rows_dst, cols_dst],
                    send_sem=s3.at[dt + 1, ds, dc], recv_sem=r3.at[dt + 1, ds, dc],
                    device_id=(g, jnp.clip(t + dt, 0, T - 1) if dt else t, s if ds == 0 else other, core),
                    device_id_type=MESH)
                there = None if dt == 0 else (t < T - 1 if dt == 1 else t > 0)
                came = None if dt == 0 else (t > 0 if dt == 1 else t < T - 1)
                landed = halo.at[core, rows_in, cols_dst]
                arrival = pltpu.make_async_copy(landed, landed, r3.at[dt + 1, ds, dc])
                rims.append((copy, there, arrival, came))

    values = conved.astype(jnp.float32).reshape(R * TC, CL, FR, CO)
    firsts = jnp.sum(jnp.sum(values, axis=0), axis=1)
    seconds = jnp.sum(jnp.sum(values * values, axis=0), axis=1)
    stats = jnp.concatenate([firsts, seconds], axis=0)
    width = C // GROUPS
    local = CO // width
    fold = (lax.broadcasted_iota(jnp.int32, (CO, 128), 0) // width
            == lax.broadcasted_iota(jnp.int32, (CO, 128), 1) % local).astype(jnp.float32).astype(jnp.bfloat16)
    spread = (lax.broadcasted_iota(jnp.int32, (128, CO), 1) // width
              == lax.broadcasted_iota(jnp.int32, (128, CO), 0) % local).astype(jnp.float32).astype(jnp.bfloat16)
    lane = lax.broadcasted_iota(jnp.int32, (2 * CL, 128), 1) // local
    kind = lax.broadcasted_iota(jnp.int32, (2 * CL, 128), 0)
    folded = sum(jnp.dot(part, fold, preferred_element_type=jnp.float32) for part in thirds(stats))
    st[c, s * T + t] = jnp.sum(jnp.where(lane == kind, folded, 0.0), axis=0, keepdims=True)
    for dt in range(T):
        for ds in range(2):
            for dc in range(2):
                if dt or ds or dc:
                    copy = pltpu.make_async_remote_copy(
                        src_ref=st.at[c, s * T + t], dst_ref=st.at[c, s * T + t],
                        send_sem=s4.at[dt, ds, dc], recv_sem=r4.at[c, s * T + t],
                        device_id=(g, lax.rem(t + dt, T), lax.rem(s + ds, 2), lax.rem(c + dc, 2)),
                        device_id_type=MESH)
                    copy.start()
                    sends.append((copy, None))
    for copy, there, _, _ in rims:
        if there is None:
            copy.start()
        else:
            pl.when(there)(copy.start)
        sends.append((copy, there))
    for copy, there in sends:
        if there is None:
            copy.wait_send()
        else:
            pl.when(there)(copy.wait_send)
    upcopy.wait()
    for dt in range(T):
        for ds in range(2):
            for dc in range(2):
                if dt or ds or dc:
                    core = lax.rem(c + dc, 2)
                    place = lax.rem(s + ds, 2) * T + lax.rem(t + dt, T)
                    pltpu.make_async_copy(st.at[core, place], st.at[core, place], r4.at[core, place]).wait()
    for k in range(2):
        pltpu.make_async_copy(par.at[k], par.at[k], r5.at[k]).wait()
    for _, _, arrival, came in rims:
        if came is None:
            arrival.wait()
        else:
            pl.when(came)(arrival.wait)

    count = float(2 * T * R * TC * FR * width)
    picks = []
    for core in range(2):
        sums = st[core, 0]
        for k in range(1, 2 * T):
            sums = sums + st[core, k]
        mean = sums / count
        squares = pltpu.roll(jnp.broadcast_to(mean, (8, 128)), 128 - CL * local, axis=1)[:1]
        factor = lax.rsqrt(squares - mean * mean + 1e-06)
        rows = jnp.where(kind < CL, jnp.broadcast_to(mean, kind.shape), jnp.broadcast_to(factor, kind.shape))
        picks.append(jnp.where(lane == kind % CL, rows, 0.0))
    both = sum(jnp.dot(part, spread, preferred_element_type=jnp.float32)
               for part in thirds(jnp.concatenate(picks, axis=0)))
    for core in range(2):
        here = c == core
        gain = jnp.where(here, vecs[1], par[0])
        shift = jnp.where(here, vecs[2], par[1])
        means, factors = both[2 * CL * core:2 * CL * core + CL], both[2 * CL * core + CL:2 * CL * (core + 1)]
        scale = factors * gain * 0.5
        offset = shift * 0.5 - means * scale
        scale, offset = (
            jnp.concatenate([jnp.broadcast_to(v[k:k + 1], (FR, CO)) for k in range(CL)], axis=0)
            for v in (scale, offset))
        for r in range(R + 2):
            for q in range(TC + 2):
                v = halo[core, r, q].astype(jnp.float32) * scale + offset
                v = v + v * jnp.tanh(v)
                keep = [s > 0] if r == 0 else [s < 1] if r == R + 1 else []
                keep += [t > 0] if q == 0 else [t < T - 1] if q == TC + 1 else []
                if keep:
                    v = jnp.where(functools.reduce(jnp.logical_and, keep), v, 0.0)
                act[r, q, :, core * CO:(core + 1) * CO] = v.astype(jnp.bfloat16)

    across = {}
    for b in range(3):
        rows = sorted({(i + b + 1) // 2 for i in range(2 * R)})
        for e in range(3):
            cols = sorted({(j + e + 1) // 2 for j in range(2 * TC)})
            lhs = jnp.concatenate([act[r, q] for r in rows for q in cols], axis=0)
            term = jnp.dot(lhs, upv[b, e], preferred_element_type=jnp.float32)
            term = term.reshape(len(rows), len(cols), frames, CO)
            for k, r in enumerate(rows):
                for j in range(2 * TC):
                    piece = term[k, cols.index((j + e + 1) // 2)]
                    across[b, r, j] = piece if e == 0 else across[b, r, j] + piece
    total = jnp.concatenate([
        across[0, (i + 1) // 2, j] + across[1, (i + 2) // 2, j] + across[2, (i + 3) // 2, j]
        for i in range(2 * R) for j in range(2 * TC)], axis=0)
    rounded = (total + vecs[3]).astype(jnp.bfloat16)
    out_ref[...] = rounded


def in_one_kernel(latents, conv_weight, conv_bias, gn_gain, gn_shift, up_weight, up_bias):
    T = lax.axis_size("tm")
    CL, per, R, W, depth = latents.shape
    cin, CO = conv_weight.shape[3:]
    TC, FR = W // T, T * per
    frames = CL * FR
    pick = jnp.asarray(gather_matrix(CL, T, per, W), jnp.bfloat16)
    rows = [v.reshape(1, CO) for v in (conv_bias, gn_gain, gn_shift, up_bias)]
    dma, vmem, anywhere = pltpu.SemaphoreType.DMA, pl.BlockSpec(memory_space=pltpu.VMEM), pl.BlockSpec(memory_space=pl.ANY)
    out = pl.pallas_call(
        functools.partial(fused, (T, R, TC, CL, FR)),
        out_shape=pltpu.VMEM((4 * R * TC * frames, CO), jnp.bfloat16),
        in_specs=[anywhere] * 8,
        out_specs=vmem,
        scratch_shapes=[
            pltpu.VMEM(pick.shape, jnp.bfloat16),
            pltpu.VMEM((4, 1, CO), jnp.float32),
            pltpu.VMEM(conv_weight.shape, jnp.bfloat16),
            pltpu.VMEM(up_weight.shape, jnp.bfloat16),
            pltpu.VMEM((T, CL, per, R + 2, W, cin), jnp.bfloat16),
            pltpu.VMEM((3, W + 2, frames, (R + 2) * cin), jnp.bfloat16),
            pltpu.VMEM((R, 2, TC * frames, CO), jnp.float32),
            pltpu.VMEM((T, R, TC * frames, CO), SEND),
            pltpu.VMEM((T, R, TC * frames, CO), SEND),
            pltpu.VMEM((2, R + 2, TC + 2, frames, CO), jnp.bfloat16),
            pltpu.VMEM((R + 2, TC + 2, frames, C), jnp.bfloat16),
            pltpu.VMEM((2, 2 * T, 1, 128), jnp.float32),
            pltpu.VMEM((2, 1, CO), jnp.float32),
            dma((7,)),
            dma((depth // cin, 2, 2)), dma((2, T)),
            dma((2, 2)), dma((T,)),
            dma((3, 2, 2)), dma((3, 2, 2)),
            dma((T, 2, 2)), dma((2, 2 * T)),
            dma((2,)), dma((2,)),
        ],
        compiler_params=pltpu.CompilerParams(collective_id=0, has_side_effects=True),
    )(latents, pick, *rows, conv_weight, up_weight)
    return out.reshape(2 * R, 2 * TC, CL, FR, CO).transpose(2, 3, 0, 1, 4)


def chosen(*operands):
    latents, conv_weight = operands[:2]
    T = lax.axis_size("tm")
    fits = (
        lax.axis_size("space") == 2 and lax.axis_size("chan") == 2 and T == 4 and latents.shape[0] == 2
        and conv_weight.shape[3] % 128 == 0 and T * latents.shape[1] == 8 and conv_weight.shape[4] == 256 and latents.shape[3] % T == 0
    )
    return (in_one_kernel if fits else on_device)(*operands)


def solution(mesh):
    placed = (
        P("groups", "tm", "space", None, "chan"),
        P(None, None, None, "tm", "chan"),
        P("chan"),
        P("chan"),
        P("chan"),
        P(None, None, None, "chan"),
        P("chan"),
    )
    return jax.shard_map(
        chosen,
        mesh=mesh,
        in_specs=placed,
        out_specs=P("groups", None, "space", "tm", "chan"),
        check_vma=False,
    )
```

```python
import functools

import jax
import jax.numpy as jnp
import numpy as np
from jax import lax
from jax.experimental import pallas as pl
from jax.experimental.pallas import tpu as pltpu
from jax.sharding import PartitionSpec as P

C = 512
GROUPS = 32


def from_behind(value, axis, steps):
    count = lax.axis_size(axis)
    pairs = [(source, (source + steps) % count) for source in range(count)]
    return lax.ppermute(value, axis, pairs)


def with_halo(block, sides, width):
    for axis, dim in sides:
        count = lax.axis_size(axis)
        forward = [(i, i + 1) for i in range(count - 1)]
        backward = [(target, source) for source, target in forward]
        low = lax.ppermute(
            lax.slice_in_dim(block, block.shape[dim] - width, None, axis=dim), axis, forward
        )
        high = lax.ppermute(lax.slice_in_dim(block, 0, width, axis=dim), axis, backward)
        block = jnp.concatenate([low, block, high], axis=dim)
    return block


def causal_frames(latents):
    clip_count = latents.shape[0]
    span_count = lax.axis_size("tm")
    span_index = lax.axis_index("tm")
    tail_frames = from_behind(latents, "tm", 1)
    clip_order = jnp.arange(clip_count, dtype=jnp.int32)
    opening = (span_index - clip_order) % span_count == 0
    tail_frames = jnp.where(
        opening[:, None, None, None, None], jnp.zeros_like(tail_frames), tail_frames
    )
    return jnp.concatenate([tail_frames, latents], axis=1)


def causal_conv(latents, conv_weight, conv_bias):
    framed = causal_frames(latents)
    bordered = with_halo(framed, (("space", 2),), 1)
    gathered = lax.all_gather(bordered, "chan", axis=4, tiled=True)
    padded = jnp.pad(gathered, ((0, 0), (0, 0), (0, 0), (1, 1), (0, 0)))
    initial = jnp.zeros(latents.shape[:4] + (conv_weight.shape[4],), jnp.float32)
    summed = initial + lax.conv_general_dilated(
        padded,
        lax.all_gather(conv_weight, "tm", axis=3, tiled=True),
        (1, 1, 1),
        "VALID",
        dimension_numbers=("NDHWC", "DHWIO", "NDHWC"),
        preferred_element_type=jnp.float32,
    )
    return (summed + conv_bias).astype(jnp.bfloat16)


def moments(block):
    clip_count, frame_count, row_count, col_count, chan_count = block.shape
    group_width = C // GROUPS
    grouped_values = block.astype(jnp.float32).reshape(
        clip_count, frame_count, row_count, col_count, chan_count // group_width, group_width
    )
    group_sums = jnp.sum(grouped_values, axis=(1, 2, 3, 5))
    squared_sums = jnp.sum(grouped_values * grouped_values, axis=(1, 2, 3, 5))
    group_sums, squared_sums = lax.psum((group_sums, squared_sums), ("tm", "space"))
    element_count = float(
        frame_count
        * row_count
        * col_count
        * group_width
        * lax.axis_size("tm")
        * lax.axis_size("space")
    )
    group_mean = group_sums / element_count
    group_variance = squared_sums / element_count - group_mean * group_mean
    return (group_mean, lax.rsqrt(group_variance + 1e-06))


def activate(block, group_mean, factor, gn_gain, gn_shift):
    clip_count, frame_count, row_count, col_count, chan_count = block.shape
    group_width = C // GROUPS
    grouped_values = block.astype(jnp.float32).reshape(
        clip_count, frame_count, row_count, col_count, chan_count // group_width, group_width
    )
    normed = (grouped_values - group_mean[:, None, None, None, :, None]) * factor[
        :, None, None, None, :, None
    ]
    normed = normed.reshape(block.shape) * gn_gain + gn_shift
    return jax.nn.silu(normed).astype(jnp.bfloat16)


def relayout(block):
    return lax.all_to_all(block, "tm", split_axis=3, concat_axis=1, tiled=True)


def widen(rimmed, up_weight, up_bias):
    gathered = lax.all_gather(rimmed, "chan", axis=4, tiled=True)
    widened = jnp.repeat(jnp.repeat(gathered, 2, axis=2), 2, axis=3)[:, :, 1:-1, 1:-1]
    clip_count, frame_count, tall_count, broad_count, depth_count = widened.shape
    flat = widened.reshape(clip_count * frame_count, tall_count, broad_count, depth_count)
    output = lax.conv_general_dilated(
        flat,
        up_weight,
        (1, 1),
        "VALID",
        dimension_numbers=("NHWC", "HWIO", "NHWC"),
        preferred_element_type=jnp.float32,
    )
    output = output + up_bias
    return output.reshape(
        clip_count, frame_count, tall_count - 2, broad_count - 2, up_weight.shape[3]
    ).astype(jnp.bfloat16)


def on_device(latents, conv_weight, conv_bias, gn_gain, gn_shift, up_weight, up_bias):
    conved = causal_conv(latents, conv_weight, conv_bias)
    tiled = relayout(conved)
    group_mean, factor = moments(tiled)
    active = activate(tiled, group_mean, factor, gn_gain, gn_shift)
    rimmed = with_halo(active, (("tm", 3), ("space", 2)), 1)
    return widen(rimmed, up_weight, up_bias)


MESH = pl.DeviceIdType.MESH
SEND = jnp.bfloat16


def gather_matrix(clips, spans, per, cols):
    frames = spans * per
    pick = np.zeros((3, cols, clips, frames, spans, clips, per, cols), np.float32)
    for a in range(3):
        for col in range(cols):
            for c in range(clips):
                for k in range(2 - a, frames):
                    slot = (k - 2 + a + c * per) % frames
                    pick[a, col, c, (k + c * per) % frames, slot // per, c, slot % per, col] = 1.0
    return pick.reshape(3, cols * clips * frames, spans * clips * per * cols)


def thirds(value):
    high = value.astype(jnp.bfloat16)
    rest = value - high.astype(jnp.float32)
    middle = rest.astype(jnp.bfloat16)
    low = (rest - middle.astype(jnp.float32)).astype(jnp.bfloat16)
    return high, middle, low


def arrived(landed, sem):
    pltpu.make_async_copy(landed, landed, sem).wait()


def fused(sizes, x_ref, pick_hbm, bias_hbm, gain_hbm, shift_hbm, upb_hbm, w_hbm, up_hbm, out_ref,
          pick_ref, vecs, wv, upv, rx, fr, kept, sb, rb, halo, act, st, par, lsem, s1, r1, s2, r2, s3, r3, s4, r4, s5, r5):
    T, R, TC, CL, FR = sizes
    g, t, s, c = (lax.axis_index(n) for n in ("groups", "tm", "space", "chan"))
    cin = rx.shape[-1]
    Q = x_ref.shape[-1] // cin
    other = 1 - s
    wcopy = pltpu.make_async_copy(w_hbm, wv, lsem.at[0])
    upcopy = pltpu.make_async_copy(up_hbm, upv, lsem.at[1])
    pcopy = pltpu.make_async_copy(pick_hbm, pick_ref, lsem.at[2])
    vcopies = [
        pltpu.make_async_copy(ref, vecs.at[k], lsem.at[3])
        for k, ref in enumerate((bias_hbm, gain_hbm, shift_hbm, upb_hbm))
    ]
    barrier = pltpu.get_barrier_semaphore()
    for dt in (1, 2, 3, 0):
        for ds in (1, 0):
            for dc in range(2):
                if dt or ds or dc:
                    pl.semaphore_signal(
                        barrier, inc=1,
                        device_id=(g, lax.rem(t + dt, T), lax.rem(s + ds, 2), lax.rem(c + dc, 2)),
                        device_id_type=MESH,
                    )
    pcopy.start()
    wcopy.start()
    for copy in vcopies:
        copy.start()
    edge = s * (R + 1)
    rx[:, :, :, pl.ds(edge, 1)] = jnp.zeros(rx.shape[:3] + (1,) + rx.shape[4:], rx.dtype)
    W = fr.shape[1] - 2
    for col in (0, W + 1):
        fr[:, col] = jnp.zeros((3,) + fr.shape[2:], fr.dtype)
    pl.semaphore_wait(barrier, 4 * T - 1)

    first = jnp.where(t <= 2 * c, 1, 0)
    for turn in range(Q):
        q = first if turn == 0 else 1 - first
        lanes = pl.ds(pl.multiple_of(q * cin, cin), cin)
        target = c * Q + q
        for dc in range(2):
            far = pltpu.make_async_remote_copy(
                src_ref=x_ref.at[:, :, pl.ds((1 - s) * (R - 1), 1), :, lanes],
                dst_ref=rx.at[t, :, :, pl.ds((1 - other) * (R + 1), 1)],
                send_sem=s1.at[0], recv_sem=r1.at[0],
                device_id=(g, target, other, lax.rem(c + dc, 2)), device_id_type=MESH)
            far.start()
        for dc in range(2):
            near = pltpu.make_async_remote_copy(
                src_ref=x_ref.at[:, :, :, :, lanes], dst_ref=rx.at[t, :, :, pl.ds(1, R)],
                send_sem=s1.at[0], recv_sem=r1.at[0],
                device_id=(g, target, s, lax.rem(c + dc, 2)), device_id_type=MESH)
            if dc:
                near.start()
            else:
                local = pltpu.make_async_copy(
                    x_ref.at[:, :, :, :, lanes], rx.at[t, :, :, pl.ds(1, R)], r1.at[0])
                pl.when(target == t)(local.start)
                pl.when(target != t)(near.start)
    upcopy.start()
    for k, ref in enumerate((gain_hbm, shift_hbm)):
        copy = pltpu.make_async_remote_copy(
            src_ref=ref, dst_ref=par.at[k], send_sem=s5.at[0], recv_sem=r5.at[0],
            device_id=(g, t, s, 1 - c), device_id_type=MESH)
        copy.start()
    pcopy.wait()
    wcopy.wait()
    arrived(vecs, lsem.at[3])
    arrived(rx.at[:, :, :, pl.ds(1 - s, R + 1)], r1.at[0])

    stacked = jnp.concatenate([rx[:, :, :, r].reshape(-1, cin) for r in range(R + 2)], axis=1)
    frames = CL * FR
    for a in range(3):
        picked = jnp.dot(pick_ref[a], stacked, preferred_element_type=jnp.float32)
        fr[a, 1:W + 1] = picked.astype(fr.dtype).reshape(W, frames, stacked.shape[1])
    taps = wv.shape[0] * wv.shape[1] * wv.shape[2]
    half = W // 2

    def send(step, u):
        side = lax.rem(t // 2 + 1 + step, 2)
        to = 3 * side if u == 0 else 1 + side
        return to, pltpu.make_async_remote_copy(
            src_ref=sb.at[to], dst_ref=rb.at[t], send_sem=s2.at[0], recv_sem=r2.at[0],
            device_id=(g, to, s, c), device_id_type=MESH)

    def halfway(step, carry):
        side = lax.rem(t // 2 + 1 + step, 2)
        lhs = jnp.concatenate([
            jnp.concatenate([
                fr[a, pl.ds(side * half + e, half), :, (r + b) * cin:(r + b + 1) * cin].reshape(half * frames, cin)
                for r in range(R)], axis=0)
            for a in range(3) for b in range(3) for e in range(3)], axis=1)
        total = jnp.dot(lhs, wv[...].reshape(taps * cin, wv.shape[4]), preferred_element_type=jnp.float32)
        parts = total.reshape(R, 2, TC * frames, wv.shape[4])
        kept[...] = parts
        for u in range(2):
            sb[side * 2 + u] = parts[:, u].astype(sb.dtype)
        for u in range(2):
            to, copy = send(step, u)
            pl.when(to != t)(copy.start)
        return carry

    lax.fori_loop(0, 2, halfway, 0)
    arrived(rb.at[pl.ds(0, T - 1)], r2.at[0])
    summed = kept[:, lax.rem(t, 2)]
    for dt in (1, 3, 2):
        source = lax.rem(t + dt, T)
        summed = summed + rb[source].astype(jnp.float32)
    summed = summed.reshape(R * TC * frames, wv.shape[4])
    conved = (summed + vecs[0]).astype(jnp.bfloat16)
    CO = conved.shape[1]
    halo[c, 1:R + 1, 1:TC + 1] = conved.reshape(R, TC, frames, CO)

    rims = []
    for dt in (0, -1, 1):
        for ds in range(2):
            for dc in range(2):
                if not (dt or ds or dc):
                    continue
                rows_src = pl.ds(1, R) if ds == 0 else pl.ds(1 + (1 - s) * (R - 1), 1)
                rows_dst = pl.ds(1, R) if ds == 0 else pl.ds((1 - other) * (R + 1), 1)
                cols_src = pl.ds(1, TC) if dt == 0 else pl.ds(TC if dt == 1 else 1, 1)
                cols_dst = pl.ds(1, TC) if dt == 0 else pl.ds(0 if dt == 1 else TC + 1, 1)
                core = lax.rem(c + dc, 2)
                copy = pltpu.make_async_remote_copy(
                    src_ref=halo.at[c, rows_src, cols_src], dst_ref=halo.at[c, rows_dst, cols_dst],
                    send_sem=s3.at[dt + 1], recv_sem=r3.at[dt + 1],
                    device_id=(g, jnp.clip(t + dt, 0, T - 1) if dt else t, s if ds == 0 else other, core),
                    device_id_type=MESH)
                there = None if dt == 0 else (t < T - 1 if dt == 1 else t > 0)
                rims.append((copy, there))

    values = conved.astype(jnp.float32).reshape(R * TC, CL, FR, CO)
    firsts = jnp.sum(jnp.sum(values, axis=0), axis=1)
    seconds = jnp.sum(jnp.sum(values * values, axis=0), axis=1)
    stats = jnp.concatenate([firsts, seconds], axis=0)
    width = C // GROUPS
    local = CO // width
    fold = (lax.broadcasted_iota(jnp.int32, (CO, 128), 0) // width
            == lax.broadcasted_iota(jnp.int32, (CO, 128), 1) % local).astype(jnp.float32).astype(jnp.bfloat16)
    spread = (lax.broadcasted_iota(jnp.int32, (128, CO), 1) // width
              == lax.broadcasted_iota(jnp.int32, (128, CO), 0) % local).astype(jnp.float32).astype(jnp.bfloat16)
    lane = lax.broadcasted_iota(jnp.int32, (2 * CL, 128), 1) // local
    kind = lax.broadcasted_iota(jnp.int32, (2 * CL, 128), 0)
    folded = sum(jnp.dot(part, fold, preferred_element_type=jnp.float32) for part in thirds(stats))
    mine = (c * 2 + s) * T + t
    st[mine] = jnp.sum(jnp.where(lane == kind, folded, 0.0), axis=0, keepdims=True)
    for dt in range(T):
        for ds in range(2):
            for dc in range(2):
                if dt or ds or dc:
                    copy = pltpu.make_async_remote_copy(
                        src_ref=st.at[mine], dst_ref=st.at[mine],
                        send_sem=s4.at[0], recv_sem=r4.at[0],
                        device_id=(g, lax.rem(t + dt, T), lax.rem(s + ds, 2), lax.rem(c + dc, 2)),
                        device_id_type=MESH)
                    copy.start()
    for copy, there in rims:
        if there is None:
            copy.start()
        else:
            pl.when(there)(copy.start)
    cells = R * TC + 2 * TC
    inner, outer = halo.at[0, pl.ds(0, 2), pl.ds(0, cells // 2)], halo.at[0, pl.ds(0, 2), pl.ds(0, R + 1)]
    local_x = c == t // 2
    pl.when(local_x)(lambda: arrived(fr.at[0, pl.ds(0, 5)], s1.at[0]))
    pl.when(jnp.logical_not(local_x))(lambda: arrived(fr.at[0, pl.ds(0, 6)], s1.at[0]))
    arrived(sb.at[pl.ds(0, T - 1)], s2.at[0])
    arrived(par, s5.at[0])
    arrived(st.at[pl.ds(0, 4 * T - 1)], s4.at[0])
    arrived(inner, s3.at[1])
    pl.when(t > 0)(lambda: arrived(outer, s3.at[0]))
    pl.when(t < T - 1)(lambda: arrived(outer, s3.at[2]))
    upcopy.wait()
    arrived(par, r5.at[0])
    arrived(st.at[pl.ds(0, 4 * T - 1)], r4.at[0])
    arrived(inner, r3.at[1])
    pl.when(t > 0)(lambda: arrived(outer, r3.at[2]))
    pl.when(t < T - 1)(lambda: arrived(outer, r3.at[0]))

    count = float(2 * T * R * TC * FR * width)
    picks = []
    for core in range(2):
        sums = st[core * 2 * T]
        for k in range(1, 2 * T):
            sums = sums + st[core * 2 * T + k]
        mean = sums / count
        squares = pltpu.roll(jnp.broadcast_to(mean, (8, 128)), 128 - CL * local, axis=1)[:1]
        factor = lax.rsqrt(squares - mean * mean + 1e-06)
        rows = jnp.where(kind < CL, jnp.broadcast_to(mean, kind.shape), jnp.broadcast_to(factor, kind.shape))
        picks.append(jnp.where(lane == kind % CL, rows, 0.0))
    both = sum(jnp.dot(part, spread, preferred_element_type=jnp.float32)
               for part in thirds(jnp.concatenate(picks, axis=0)))
    for core in range(2):
        here = c == core
        gain = jnp.where(here, vecs[1], par[0])
        shift = jnp.where(here, vecs[2], par[1])
        means, factors = both[2 * CL * core:2 * CL * core + CL], both[2 * CL * core + CL:2 * CL * (core + 1)]
        scale = factors * gain * 0.5
        offset = shift * 0.5 - means * scale
        scale, offset = (
            jnp.concatenate([jnp.broadcast_to(v[k:k + 1], (FR, CO)) for k in range(CL)], axis=0)
            for v in (scale, offset))
        for r in range(R + 2):
            for q in range(TC + 2):
                v = halo[core, r, q].astype(jnp.float32) * scale + offset
                v = v + v * jnp.tanh(v)
                keep = [s > 0] if r == 0 else [s < 1] if r == R + 1 else []
                keep += [t > 0] if q == 0 else [t < T - 1] if q == TC + 1 else []
                if keep:
                    v = jnp.where(functools.reduce(jnp.logical_and, keep), v, 0.0)
                act[r, q, :, core * CO:(core + 1) * CO] = v.astype(jnp.bfloat16)

    across = {}
    for b in range(3):
        rows = sorted({(i + b + 1) // 2 for i in range(2 * R)})
        for e in range(3):
            cols = sorted({(j + e + 1) // 2 for j in range(2 * TC)})
            lhs = jnp.concatenate([act[r, q] for r in rows for q in cols], axis=0)
            term = jnp.dot(lhs, upv[b, e], preferred_element_type=jnp.float32)
            term = term.reshape(len(rows), len(cols), frames, CO)
            for k, r in enumerate(rows):
                for j in range(2 * TC):
                    piece = term[k, cols.index((j + e + 1) // 2)]
                    across[b, r, j] = piece if e == 0 else across[b, r, j] + piece
    total = jnp.concatenate([
        across[0, (i + 1) // 2, j] + across[1, (i + 2) // 2, j] + across[2, (i + 3) // 2, j]
        for i in range(2 * R) for j in range(2 * TC)], axis=0)
    rounded = (total + vecs[3]).astype(jnp.bfloat16)
    out_ref[...] = rounded


def in_one_kernel(latents, conv_weight, conv_bias, gn_gain, gn_shift, up_weight, up_bias):
    T = lax.axis_size("tm")
    CL, per, R, W, depth = latents.shape
    cin, CO = conv_weight.shape[3:]
    TC, FR = W // T, T * per
    frames = CL * FR
    pick = jnp.asarray(gather_matrix(CL, T, per, W), jnp.bfloat16)
    rows = [v.reshape(1, CO) for v in (conv_bias, gn_gain, gn_shift, up_bias)]
    dma, vmem, anywhere = pltpu.SemaphoreType.DMA, pl.BlockSpec(memory_space=pltpu.VMEM), pl.BlockSpec(memory_space=pl.ANY)
    out = pl.pallas_call(
        functools.partial(fused, (T, R, TC, CL, FR)),
        out_shape=pltpu.VMEM((4 * R * TC * frames, CO), jnp.bfloat16),
        in_specs=[anywhere] * 8,
        out_specs=vmem,
        scratch_shapes=[
            pltpu.VMEM(pick.shape, jnp.bfloat16),
            pltpu.VMEM((4, 1, CO), jnp.float32),
            pltpu.VMEM(conv_weight.shape, jnp.bfloat16),
            pltpu.VMEM(up_weight.shape, jnp.bfloat16),
            pltpu.VMEM((T, CL, per, R + 2, W, cin), jnp.bfloat16),
            pltpu.VMEM((3, W + 2, frames, (R + 2) * cin), jnp.bfloat16),
            pltpu.VMEM((R, 2, TC * frames, CO), jnp.float32),
            pltpu.VMEM((T, R, TC * frames, CO), SEND),
            pltpu.VMEM((T, R, TC * frames, CO), SEND),
            pltpu.VMEM((2, R + 2, TC + 2, frames, CO), jnp.bfloat16),
            pltpu.VMEM((R + 2, TC + 2, frames, C), jnp.bfloat16),
            pltpu.VMEM((4 * T, 1, 128), jnp.float32),
            pltpu.VMEM((2, 1, CO), jnp.float32),
            dma((4,)),
            dma((1,)), dma((1,)),
            dma((1,)), dma((1,)),
            dma((3,)), dma((3,)),
            dma((1,)), dma((1,)),
            dma((1,)), dma((1,)),
        ],
        compiler_params=pltpu.CompilerParams(collective_id=0, has_side_effects=True),
    )(latents, pick, *rows, conv_weight, up_weight)
    return out.reshape(2 * R, 2 * TC, CL, FR, CO).transpose(2, 3, 0, 1, 4)


def chosen(*operands):
    latents, conv_weight = operands[:2]
    T = lax.axis_size("tm")
    fits = (
        lax.axis_size("space") == 2 and lax.axis_size("chan") == 2 and T == 4 and latents.shape[0] == 2
        and conv_weight.shape[3] % 128 == 0 and T * latents.shape[1] == 8 and conv_weight.shape[4] == 256 and latents.shape[2:4] == (2, 2 * T)
        and latents.shape[1] == 2 and latents.shape[4] == 2 * conv_weight.shape[3] == 256
    )
    return (in_one_kernel if fits else on_device)(*operands)


def solution(mesh):
    placed = (
        P("groups", "tm", "space", None, "chan"),
        P(None, None, None, "tm", "chan"),
        P("chan"),
        P("chan"),
        P("chan"),
        P(None, None, None, "chan"),
        P("chan"),
    )
    return jax.shard_map(
        chosen,
        mesh=mesh,
        in_specs=placed,
        out_specs=P("groups", None, "space", "tm", "chan"),
        check_vma=False,
    )
```
